32 devices in a mesh: blk: 8 (over y, x, core), rep: 4 (over z).
Axes of the slice: x: 2, y: 2, z: 4, core: 2. Of those that a mesh axis runs over, the one named last changes fastest.
Arguments:
- coords: float32 [3, 1200, 2048], P(None, 'rep', 'blk'), may hold values from -40 to 40
- frame_count: int32 [8], P('blk'), may hold values from 64 to 256, as said below
Outputs:
- deviation_behind: float32 [3, 2048, 256], P(None, ('blk', 'rep'))
- deviation_ahead: float32 [3, 2048, 256], P(None, ('blk', 'rep'))
The draws below stay inside these ranges and needn't reach their ends.
Inputs may be any that keep to these rules, and one draw needn't show every extreme that they name: `frame_count`: at least one block is full and at least one holds exactly 64 frames.
All inputs are finite; a program needn't handle non-finite values.
Results may differ from the reference program's by a relative error of at most 0.0003.
Values sent between devices are 32-bit elements; how exact they have to be, the bound alone decides.
A program may use at most 64 MiB of HBM per device.

```python
import math
import jax
import jax.numpy as jnp
from jax import lax

FR_BLK = 256
NATOM = 1200
ROUNDS = 3
NEWTON = 4
BLOCKS = 8
FRAMES = 2048


def rotation_tables(quat):
    norm_q = jnp.sqrt(jnp.sum(quat * quat, axis=0))
    w_part = quat[0] / norm_q
    x_part = quat[1] / norm_q
    y_part = quat[2] / norm_q
    z_part = quat[3] / norm_q
    row_one = jnp.stack([1.0 - 2.0 * (y_part * y_part + z_part * z_part), 2.0 * (x_part * y_part - w_part * z_part), 2.0 * (x_part * z_part + w_part * y_part)], 0)
    row_two = jnp.stack([2.0 * (x_part * y_part + w_part * z_part), 1.0 - 2.0 * (x_part * x_part + z_part * z_part), 2.0 * (y_part * z_part - w_part * x_part)], 0)
    row_three = jnp.stack([2.0 * (x_part * z_part - w_part * y_part), 2.0 * (y_part * z_part + w_part * x_part), 1.0 - 2.0 * (x_part * x_part + y_part * y_part)], 0)
    return jnp.stack([row_one, row_two, row_three], 0)


def draw_coords(key, part):
    pieces = jax.random.split(key, 5)
    scales = jnp.array([1.5, 1.0, 0.6], jnp.float32).reshape(3, 1)
    structure = jax.random.normal(pieces[0], (3, NATOM), jnp.float32) * scales
    quat = jax.random.normal(pieces[4], (4, FRAMES), jnp.float32)
    rotation = rotation_tables(quat)
    rotated = jnp.einsum('klf,la->kaf', rotation, structure)
    amplitude = jnp.exp(jax.random.uniform(pieces[1], (1, 1, FRAMES), jnp.float32, math.log(0.7), math.log(2.5)))
    noise = jax.random.normal(pieces[2], (3, NATOM, FRAMES), jnp.float32)
    offset = 3.0 * jax.random.normal(pieces[3], (3, 1, FRAMES), jnp.float32)
    return jnp.clip(rotated + amplitude * noise + offset, -40.0, 40.0).astype(jnp.float32)


def draw_frame_count(key, part):
    first, second = jax.random.split(key)
    counts = jax.random.randint(first, (BLOCKS,), FR_BLK // 4, FR_BLK + 1, jnp.int32)
    chosen = jax.random.randint(second, (), 0, BLOCKS, jnp.int32)
    shortest = (chosen + 1) % BLOCKS
    indices = jnp.arange(BLOCKS, dtype=jnp.int32)
    counts = jnp.where(indices == shortest, FR_BLK // 4, counts)
    return jnp.where(indices == chosen, FR_BLK, counts).astype(jnp.int32)


def setup_inputs(seed: int = 0) -> dict:
    keys = jax.random.split(jax.random.key(seed), 3)
    coords = draw_coords(jax.random.fold_in(keys[2], 71), 0)
    frame_count = draw_frame_count(jax.random.fold_in(keys[2], 71), 0)
    return dict(coords=coords, frame_count=frame_count)


def pair_minor(upper, lower, left, right):
    return upper[left] * lower[right] - upper[right] * lower[left]


def deviation(covariance, own_sq, other_sq):
    m = [[covariance[first, :, second, :] for second in range(3)] for first in range(3)]
    keyed = [
        [m[0][0] + m[1][1] + m[2][2], m[1][2] - m[2][1], m[2][0] - m[0][2], m[0][1] - m[1][0]],
        [m[1][2] - m[2][1], m[0][0] - m[1][1] - m[2][2], m[0][1] + m[1][0], m[2][0] + m[0][2]],
        [m[2][0] - m[0][2], m[0][1] + m[1][0], -m[0][0] + m[1][1] - m[2][2], m[1][2] + m[2][1]],
        [m[0][1] - m[1][0], m[2][0] + m[0][2], m[1][2] + m[2][1], -m[0][0] - m[1][1] + m[2][2]],
    ]
    top_one, top_two, low_one, low_two = keyed
    det_key = (pair_minor(top_one, top_two, 0, 1) * pair_minor(low_one, low_two, 2, 3)
               - pair_minor(top_one, top_two, 0, 2) * pair_minor(low_one, low_two, 1, 3)
               + pair_minor(top_one, top_two, 0, 3) * pair_minor(low_one, low_two, 1, 2)
               + pair_minor(top_one, top_two, 1, 2) * pair_minor(low_one, low_two, 0, 3)
               - pair_minor(top_one, top_two, 1, 3) * pair_minor(low_one, low_two, 0, 2)
               + pair_minor(top_one, top_two, 2, 3) * pair_minor(low_one, low_two, 0, 1))
    det_three = (m[0][0] * (m[1][1] * m[2][2] - m[1][2] * m[2][1])
                 - m[0][1] * (m[1][0] * m[2][2] - m[1][2] * m[2][0])
                 + m[0][2] * (m[1][0] * m[2][1] - m[1][1] * m[2][0]))
    square_sum = m[0][0] * m[0][0]
    for first in range(3):
        for second in range(3):
            if first + second > 0:
                square_sum = square_sum + m[first][second] * m[first][second]
    second_coef = -2.0 * square_sum
    first_coef = -8.0 * det_three
    total = own_sq[:, None] + other_sq[None, :]
    largest = 0.5 * total
    for newton_step in range(NEWTON):
        squared = largest * largest
        polynomial = squared * squared + second_coef * squared + first_coef * largest + det_key
        derivative = 4.0 * squared * largest + 2.0 * second_coef * largest + first_coef
        largest = largest - polynomial / derivative
    return total - 2.0 * largest


def reference(coords, frame_count):
    centroid = jnp.sum(coords, axis=1, keepdims=True) / NATOM
    centered = coords - centroid
    self_sq = jnp.sum(centered * centered, axis=(0, 1)) / NATOM
    blocked = centered.reshape(3, NATOM, BLOCKS, FR_BLK)
    block_sq = self_sq.reshape(BLOCKS, FR_BLK)
    valid = jnp.arange(FR_BLK, dtype=jnp.int32)[None, :] < frame_count[:, None]
    behind_list = []
    ahead_list = []
    for distance in range(1, ROUNDS + 1):
        def one_pair(block, shift_by=distance):
            partner = ((block - shift_by) % BLOCKS).astype(jnp.int32)
            own_block = lax.dynamic_index_in_dim(blocked, block, 2, keepdims=False)
            partner_block = lax.dynamic_index_in_dim(blocked, partner, 2, keepdims=False)
            covariance = lax.dot_general(own_block, partner_block, (((1,), (1,)), ((), ())),
                                         precision=lax.Precision.HIGHEST) / NATOM
            own_sq = lax.dynamic_index_in_dim(block_sq, block, 0, keepdims=False)
            other_sq = lax.dynamic_index_in_dim(block_sq, partner, 0, keepdims=False)
            own_valid = lax.dynamic_index_in_dim(valid, block, 0, keepdims=False)
            other_valid = lax.dynamic_index_in_dim(valid, partner, 0, keepdims=False)
            mask = own_valid[:, None] & other_valid[None, :]
            return jnp.where(mask, deviation(covariance, own_sq, other_sq), 0.0)

        pair_blocks = lax.map(one_pair, jnp.arange(BLOCKS, dtype=jnp.int32))
        behind_list.append(pair_blocks.reshape(FRAMES, FR_BLK))
        rolled = jnp.roll(pair_blocks, -distance, axis=0)
        ahead_list.append(jnp.transpose(rolled, (0, 2, 1)).reshape(FRAMES, FR_BLK))
    return jnp.stack(behind_list, 0), jnp.stack(ahead_list, 0)
```

```python
import functools

import jax
import jax.numpy as jnp
from jax import lax
from jax.experimental import pallas as pl
from jax.experimental.pallas import tpu as pltpu
from jax.sharding import PartitionSpec as P

ROUNDS = 3
NEWTON = 4
MESH = pl.DeviceIdType.MESH

FIRST = (
    ((1, 1), (0, 1)),
    ((1, 1), (0, -1), (0, 1)),
    ((0, -1), (1, 1), (1, -1)),
    ((0, -1), (1, -1)),
)
ARRIVE = (
    ((1, 0, 0), (2, 0, 0), (3, 0, 0)),
    ((0, 1, 1), (2, 0, -1), (0, 0, 1), (2, 1, 0), (3, 0, -1), (3, 1, 0)),
    ((3, 0, -1), (1, 1, 1), (3, 1, -1), (1, 0, 0), (0, 1, 1), (0, 0, 0)),
    ((2, 1, 0), (1, 1, 0), (0, 1, 0)),
)


def pair_minor(upper, lower, left, right):
    return upper[left] * lower[right] - upper[right] * lower[left]


def deviation(m, total):
    keyed = [
        [m[0][0] + m[1][1] + m[2][2], m[1][2] - m[2][1], m[2][0] - m[0][2], m[0][1] - m[1][0]],
        [m[1][2] - m[2][1], m[0][0] - m[1][1] - m[2][2], m[0][1] + m[1][0], m[2][0] + m[0][2]],
        [m[2][0] - m[0][2], m[0][1] + m[1][0], -m[0][0] + m[1][1] - m[2][2], m[1][2] + m[2][1]],
        [m[0][1] - m[1][0], m[2][0] + m[0][2], m[1][2] + m[2][1], -m[0][0] - m[1][1] + m[2][2]],
    ]
    top_one, top_two, low_one, low_two = keyed
    det_key = (
        pair_minor(top_one, top_two, 0, 1) * pair_minor(low_one, low_two, 2, 3)
        - pair_minor(top_one, top_two, 0, 2) * pair_minor(low_one, low_two, 1, 3)
        + pair_minor(top_one, top_two, 0, 3) * pair_minor(low_one, low_two, 1, 2)
        + pair_minor(top_one, top_two, 1, 2) * pair_minor(low_one, low_two, 0, 3)
        - pair_minor(top_one, top_two, 1, 3) * pair_minor(low_one, low_two, 0, 2)
        + pair_minor(top_one, top_two, 2, 3) * pair_minor(low_one, low_two, 0, 1)
    )
    det_three = (
        m[0][0] * (m[1][1] * m[2][2] - m[1][2] * m[2][1])
        - m[0][1] * (m[1][0] * m[2][2] - m[1][2] * m[2][0])
        + m[0][2] * (m[1][0] * m[2][1] - m[1][1] * m[2][0])
    )
    square_sum = m[0][0] * m[0][0]
    for first in range(3):
        for second in range(3):
            if first + second > 0:
                square_sum = square_sum + m[first][second] * m[first][second]
    second_coef = -2.0 * square_sum
    first_coef = -8.0 * det_three
    largest = 0.5 * total
    for newton_step in range(NEWTON):
        squared = largest * largest
        polynomial = squared * squared + second_coef * squared + first_coef * largest + det_key
        derivative = 4.0 * squared * largest + 2.0 * second_coef * largest + first_coef
        largest = largest - polynomial / derivative
    return total - 2.0 * largest


def split(value):
    high = value.astype(jnp.bfloat16)
    low = (value - high.astype(jnp.float32)).astype(jnp.bfloat16)
    return high, low


def kernel(n, reps, coords, cnt, behind, ahead, own, part, pcnt, full, fth, ftl, gh, gl, cov,
           fsq, dev, devt, zs, zr, xs, pr, cs, cr, os, br, ar, ls):
    b = lax.axis_index("blk")
    z = lax.axis_index("rep")
    par = lax.rem(b, 2)
    atoms = coords.shape[1]
    half = coords.shape[2] // 2
    quarter = half // 2
    pitch = (atoms + 15) // 16 * 16
    natom = atoms * reps
    fh = z // 2
    gside = lax.rem(z, 2)

    def at(step):
        return lax.rem(b + step + n, n)

    barrier = pltpu.get_barrier_semaphore()
    for step in range(-ROUNDS, ROUNDS + 1):
        for turn in range(reps):
            if step or turn:
                pl.semaphore_signal(barrier, inc=1, device_id=(at(step), lax.rem(z + turn, reps)),
                                    device_id_type=MESH)
    pl.semaphore_wait(barrier, (2 * ROUNDS + 1) * reps - 1)

    def remote(src, dst, send, recv, where):
        return pltpu.make_async_remote_copy(src_ref=src, dst_ref=dst, send_sem=send, recv_sem=recv,
                                            device_id=where, device_id_type=MESH)

    def along(me, s, h, k, step):
        src = coords.at[k, :, pl.ds(h * half, half)] if s == me else own.at[s, h, k]
        return remote(src, own.at[s, h, k], zs.at[(step + 1) // 2, s, h, k], zr.at[s, h, k],
                      (b, z + step))

    def across(me, s, k):
        h = me % 2
        src = coords.at[k, :, pl.ds(h * half, half)] if s == me else own.at[s, h, k]
        slot = 2 * par
        return (
            remote(src, part.at[1, s, k], xs.at[0, s, k], pr.at[1, s, k], (at(2), z)),
            remote(src, part.at[slot, s, k], xs.at[1, s, k], pr.at[slot, s, k], (at(1 + slot), z)),
        )

    def relay(s, k):
        slot = 2 - 2 * par
        return remote(part.at[1, s, k], part.at[slot, s, k], xs.at[2, s, k], pr.at[slot, s, k],
                      (at(1 - 2 * par), z))

    def count_copy(d):
        return remote(cnt, pcnt.at[d], cs.at[d], cr.at[d], (at(d + 1), z))

    def local():
        return pltpu.make_async_copy(coords.at[:, :, pl.ds(pl.multiple_of(fh * half, half), half)],
                                     own.at[z, fh], ls)

    def behind_copy(d):
        other = pl.multiple_of(quarter * (1 - gside), quarter)
        cols = pl.ds(pl.multiple_of(gside * half, half), half)
        return remote(dev.at[d, pl.ds(other, quarter)], behind.at[d, :, cols], os.at[d, 0],
                      br.at[d], (b, z + 1 - 2 * gside))

    def ahead_copy(d, j):
        cols = pl.ds(pl.multiple_of(fh * half, half), half)
        return remote(devt.at[d, pl.ds(j * quarter, quarter)], ahead.at[d, :, cols],
                      os.at[d, 1 + j], ar.at[d, fh], (lax.rem(b - 1 - d + n, n), 2 * gside + j))

    def program(me):
        for h, step in FIRST[me]:
            for k in range(3):
                along(me, me, h, k, step).start()
        for k in range(3):
            for copy in across(me, me, k):
                copy.start()
        local().start()
        for d in range(ROUNDS):
            count_copy(d).start()
        pending = [me]
        for s, h, step in ARRIVE[me]:
            fresh = h == me % 2
            for k in range(3):
                zr_wait(s, h, k)
                if step:
                    along(me, s, h, k, step).start()
                if fresh:
                    for copy in across(me, s, k):
                        copy.start()
            if fresh:
                due = pending.pop(0)
                for k in range(3):
                    pr_wait(1, due, k)
                    relay(due, k).start()
                pending.append(s)
        for due in pending:
            for k in range(3):
                pr_wait(1, due, k)
                relay(due, k).start()

    def zr_wait(s, h, k):
        remote(own.at[s, h, k], own.at[s, h, k], zs.at[0, s, h, k], zr.at[s, h, k],
               (b, lax.rem(z + 1, reps))).wait_recv()

    def pr_wait(d, s, k):
        remote(part.at[d, s, k], part.at[d, s, k], xs.at[0, s, k], pr.at[d, s, k],
               (b, lax.rem(z + 1, reps))).wait_recv()

    def finish(me):
        for h, step in FIRST[me]:
            for k in range(3):
                along(me, me, h, k, step).wait_send()
        for s, h, step in ARRIVE[me]:
            if step:
                for k in range(3):
                    along(me, s, h, k, step).wait_send()
        for s in range(reps):
            for k in range(3):
                for copy in across(me, s, k):
                    copy.wait_send()
                relay(s, k).wait_send()

    for me in range(reps):
        @pl.when(z == me)
        def _(me=me):
            program(me)

    local().wait()
    full[...] = jnp.zeros_like(full)
    gh[...] = jnp.zeros_like(gh)
    gl[...] = jnp.zeros_like(gl)
    fsq[...] = jnp.zeros_like(fsq)
    for k in range(3):
        mean = sum(jnp.sum(own[s, fh, k], axis=0, keepdims=True) for s in range(reps)) / natom
        for s in range(reps):
            full[s * pitch:s * pitch + atoms, :] = own[s, fh, k] - mean
        turned = full[...].T
        fsq[...] += jnp.broadcast_to(jnp.sum(turned * turned, axis=1, keepdims=True), fsq.shape)
        high, low = split(turned)
        fth[k * half:(k + 1) * half, :] = high
        ftl[k * half:(k + 1) * half, :] = low
    fsq[...] = fsq[...] / natom
    for d in range(ROUNDS):
        count_copy(d).wait_recv()

    def block(turn, carry):
        d = lax.rem(turn + 1, ROUNDS)

        @pl.when(d != 1)
        def _():
            for s in range(reps):
                for k in range(3):
                    pr_wait(d, s, k)

        square = jnp.zeros((1, half), jnp.float32)
        for k in range(3):
            mean = sum(jnp.sum(part[d, s, k], axis=0, keepdims=True) for s in range(reps)) / natom
            for s in range(reps):
                centered = part[d, s, k] - mean
                square = square + jnp.sum(centered * centered, axis=0, keepdims=True)
                high, low = split(centered)
                gh[s * pitch:s * pitch + atoms, k * half:(k + 1) * half] = high
                gl[s * pitch:s * pitch + atoms, k * half:(k + 1) * half] = low
        square = square / natom
        product = functools.partial(jnp.dot, preferred_element_type=jnp.float32)
        cov[...] = (product(fth[...], gh[...]) + product(fth[...], gl[...])
                    + product(ftl[...], gh[...])) / natom
        rows = 16

        def chunk(i, inner):
            r = pl.multiple_of(i * rows, rows)
            m = [[cov[pl.ds(k * half + r, rows), l * half:(l + 1) * half] for l in range(3)]
                 for k in range(3)]
            total = fsq[pl.ds(r, rows), :] + square
            frame = fh * half + r + lax.broadcasted_iota(jnp.int32, (rows, half), 0)
            other = gside * half + lax.broadcasted_iota(jnp.int32, (rows, half), 1)
            mask = (frame < cnt[0:1, :]) & (other < pcnt[d, 0:1, :])
            dev[d, pl.ds(r, rows), :] = jnp.where(mask, deviation(m, total), 0.0)
            return inner

        lax.fori_loop(0, half // rows, chunk, 0)
        behind_copy(d).start()
        devt[d] = dev[d].T
        cols = pl.ds(pl.multiple_of(gside * half, half), half)
        behind[d, :, cols] = dev[d, pl.ds(pl.multiple_of(quarter * gside, quarter), quarter), :]
        for j in range(2):
            ahead_copy(d, j).start()
        return carry

    lax.fori_loop(0, ROUNDS, block, 0)
    for me in range(reps):
        @pl.when(z == me)
        def _(me=me):
            finish(me)
    for d in range(ROUNDS):
        count_copy(d).wait_send()
        behind_copy(d).wait()
        for j in range(2):
            ahead_copy(d, j).wait_send()
            remote(devt.at[d, pl.ds(0, quarter)], ahead.at[d, :, pl.ds(j * half, half)],
                   os.at[d, 1], ar.at[d, j], (at(1), z)).wait_recv()


def shards(n, reps, coords, frame_count):
    atoms, frames = coords.shape[1], coords.shape[2]
    half = frames // 2
    depth = ((atoms + 15) // 16 * 16 * reps + 127) // 128 * 128
    counts = jnp.broadcast_to(frame_count.astype(jnp.int32)[:, None], (8, half))
    f32, bf16 = jnp.float32, jnp.bfloat16
    dma = pltpu.SemaphoreType.DMA
    vmem = pl.BlockSpec(memory_space=pltpu.VMEM)
    result = jax.ShapeDtypeStruct((ROUNDS, frames // reps, frames), f32)
    return pl.pallas_call(
        functools.partial(kernel, n, reps),
        out_shape=(result, result),
        in_specs=[pl.BlockSpec(memory_space=pl.ANY), vmem],
        out_specs=(vmem, vmem),
        scratch_shapes=[
            pltpu.VMEM((reps, 2, 3, atoms, half), f32),
            pltpu.VMEM((ROUNDS, reps, 3, atoms, half), f32),
            pltpu.VMEM((ROUNDS, 8, half), jnp.int32),
            pltpu.VMEM((depth, half), f32),
            pltpu.VMEM((3 * half, depth), bf16),
            pltpu.VMEM((3 * half, depth), bf16),
            pltpu.VMEM((depth, 3 * half), bf16),
            pltpu.VMEM((depth, 3 * half), bf16),
            pltpu.VMEM((3 * half, 3 * half), f32),
            pltpu.VMEM((half, half), f32),
            pltpu.VMEM((ROUNDS, half, half), f32),
            pltpu.VMEM((ROUNDS, half, half), f32),
            dma((2, reps, 2, 3)),
            dma((reps, 2, 3)),
            dma((3, reps, 3)),
            dma((ROUNDS, reps, 3)),
            dma((ROUNDS,)),
            dma((ROUNDS,)),
            dma((ROUNDS, 3)),
            dma((ROUNDS,)),
            dma((ROUNDS, 2)),
            dma(()),
        ],
        compiler_params=pltpu.CompilerParams(collective_id=0, has_side_effects=True),
    )(coords, counts)


def solution(mesh):
    in_specs = (P(None, "rep", "blk"), P("blk"))
    out_specs = (P(None, ("blk", "rep"), None), P(None, ("blk", "rep"), None))
    body = functools.partial(shards, mesh.shape["blk"], mesh.shape["rep"])
    return jax.shard_map(body, mesh=mesh, in_specs=in_specs, out_specs=out_specs, check_vma=False)
```

```python
import functools

import jax
import jax.numpy as jnp
from jax import lax
from jax.experimental import pallas as pl
from jax.experimental.pallas import tpu as pltpu
from jax.sharding import PartitionSpec as P

ROUNDS = 3
NEWTON = 4
MESH = pl.DeviceIdType.MESH

ALL = (0, 1, 2)
FIRST = (
    ((1, 1, ALL), (0, 1, ALL)),
    ((1, 1, ALL), (0, -1, ALL), (0, 1, (0,))),
    ((0, -1, ALL), (1, 1, ALL), (1, -1, (0,))),
    ((0, -1, ALL), (1, -1, ALL)),
)
LATE = ((), ((0, 1, (1, 2)),), ((1, -1, (1, 2)),), ())
ARRIVE = (
    (((1, 0, 0),), ((2, 0, 0),), ((3, 0, 0),)),
    (((2, 0, -1), (0, 1, 1)), ((3, 0, -1), (0, 0, 1))),
    (((1, 1, 1), (3, 0, -1)), ((0, 1, 1), (3, 1, -1))),
    (((2, 1, 0),), ((1, 1, 0),), ((0, 1, 0),)),
)
LAST = ((), ((2, 1), (3, 1)), ((1, 0), (0, 0)), ())


def pair_minor(upper, lower, left, right):
    return upper[left] * lower[right] - upper[right] * lower[left]


def deviation(m, total):
    keyed = [
        [m[0][0] + m[1][1] + m[2][2], m[1][2] - m[2][1], m[2][0] - m[0][2], m[0][1] - m[1][0]],
        [m[1][2] - m[2][1], m[0][0] - m[1][1] - m[2][2], m[0][1] + m[1][0], m[2][0] + m[0][2]],
        [m[2][0] - m[0][2], m[0][1] + m[1][0], -m[0][0] + m[1][1] - m[2][2], m[1][2] + m[2][1]],
        [m[0][1] - m[1][0], m[2][0] + m[0][2], m[1][2] + m[2][1], -m[0][0] - m[1][1] + m[2][2]],
    ]
    top_one, top_two, low_one, low_two = keyed
    det_key = (
        pair_minor(top_one, top_two, 0, 1) * pair_minor(low_one, low_two, 2, 3)
        - pair_minor(top_one, top_two, 0, 2) * pair_minor(low_one, low_two, 1, 3)
        + pair_minor(top_one, top_two, 0, 3) * pair_minor(low_one, low_two, 1, 2)
        + pair_minor(top_one, top_two, 1, 2) * pair_minor(low_one, low_two, 0, 3)
        - pair_minor(top_one, top_two, 1, 3) * pair_minor(low_one, low_two, 0, 2)
        + pair_minor(top_one, top_two, 2, 3) * pair_minor(low_one, low_two, 0, 1)
    )
    det_three = (
        m[0][0] * (m[1][1] * m[2][2] - m[1][2] * m[2][1])
        - m[0][1] * (m[1][0] * m[2][2] - m[1][2] * m[2][0])
        + m[0][2] * (m[1][0] * m[2][1] - m[1][1] * m[2][0])
    )
    square_sum = m[0][0] * m[0][0]
    for first in range(3):
        for second in range(3):
            if first + second > 0:
                square_sum = square_sum + m[first][second] * m[first][second]
    second_coef = -2.0 * square_sum
    first_coef = -8.0 * det_three
    largest = 0.5 * total
    for newton_step in range(NEWTON):
        squared = largest * largest
        polynomial = squared * squared + second_coef * squared + first_coef * largest + det_key
        derivative = 4.0 * squared * largest + 2.0 * second_coef * largest + first_coef
        largest = largest - polynomial / derivative
    return total - 2.0 * largest


def split(value):
    high = value.astype(jnp.bfloat16)
    low = (value - high.astype(jnp.float32)).astype(jnp.bfloat16)
    return high, low


def kernel(n, reps, coords, cnt, behind, ahead, own, part, pcnt, full, fth, ftl, gh, gl, cov,
           fsq, dev, devt, zs, zr, xs, pr, cs, cr, os, br, ar, ls):
    b = lax.axis_index("blk")
    z = lax.axis_index("rep")
    par = lax.rem(b, 2)
    bent = lax.rem(b // 2, 2) * par == 1
    bends = lax.rem(b // 2, 2) * (1 - par) == 1
    atoms = coords.shape[1]
    half = coords.shape[2] // 2
    quarter = half // 2
    pitch = (atoms + 15) // 16 * 16
    natom = atoms * reps
    fh = lax.rem(z, 2)
    gside = z // 2

    def at(step):
        return lax.rem(b + step + n, n)

    barrier = pltpu.get_barrier_semaphore()
    for step in range(-ROUNDS, ROUNDS + 1):
        if step:
            pl.semaphore_signal(barrier, inc=1, device_id=(at(step), z), device_id_type=MESH)

    @pl.when(z > 0)
    def _():
        pl.semaphore_signal(barrier, inc=1, device_id=(b, z - 1), device_id_type=MESH)

    @pl.when(z < reps - 1)
    def _():
        pl.semaphore_signal(barrier, inc=1, device_id=(b, z + 1), device_id_type=MESH)

    inner = jnp.minimum(z, 1) * jnp.minimum(reps - 1 - z, 1)
    pl.semaphore_wait(barrier, 2 * ROUNDS + 1 + inner)

    def remote(src, dst, send, recv, where):
        return pltpu.make_async_remote_copy(src_ref=src, dst_ref=dst, send_sem=send, recv_sem=recv,
                                            device_id=where, device_id_type=MESH)

    def along(me, s, h, k, step):
        src = coords.at[k, :, pl.ds(h * half, half)] if s == me else own.at[s, h, k]
        return remote(src, own.at[s, h, k], zs.at[(step + 1) // 2, s, h, k], zr.at[s, h, k],
                      (b, z + step))

    def across(me, s, k):
        h = me // 2
        src = coords.at[k, :, pl.ds(h * half, half)] if s == me else own.at[s, h, k]
        slot = 2 * par
        return (
            remote(src, part.at[slot, s, k], xs.at[1, s, k], pr.at[slot, s, k], (at(1 + slot), z)),
            remote(src, part.at[1, s, k], xs.at[0, s, k], pr.at[1, s, k], (at(2), z)),
        )

    def across_start(me, s, k):
        first, second = across(me, s, k)
        first.start()

        @pl.when(jnp.logical_not(bent))
        def _():
            second.start()

    def bend(s, k):
        return remote(part.at[2, s, k], part.at[1, s, k], xs.at[3, s, k], pr.at[1, s, k],
                      (at(-1), z))

    def relay(s, k):
        slot = 2 - 2 * par
        return remote(part.at[1, s, k], part.at[slot, s, k], xs.at[2, s, k], pr.at[slot, s, k],
                      (at(1 - 2 * par), z))

    def pass_on(s):
        @pl.when(bends)
        def _():
            for k in range(3):
                pr_wait(2, s, k)
                bend(s, k).start()

        for k in range(3):
            pr_wait(1, s, k)
            relay(s, k).start()

    def count_copy(d):
        return remote(cnt, pcnt.at[d], cs.at[d], cr.at[d], (at(d + 1), z))

    def local():
        return pltpu.make_async_copy(coords.at[:, :, pl.ds(pl.multiple_of(fh * half, half), half)],
                                     own.at[z, fh], ls)

    cols = pl.ds(pl.multiple_of(gside * half, half), half)

    def behind_copy(d, j):
        return remote(dev.at[d, pl.ds(j * quarter, quarter)], behind.at[d, :, cols],
                      os.at[d, 2 + j], br.at[d, gside], (b, 2 * fh + j))

    def ahead_copy(d, j):
        mine = pl.ds(pl.multiple_of(fh * half, half), half)
        return remote(devt.at[d, pl.ds(j * quarter, quarter)], ahead.at[d, :, mine],
                      os.at[d, j], ar.at[d, fh], (lax.rem(b - 1 - d + n, n), 2 * gside + j))

    def program(me):
        for h, step, parts in FIRST[me]:
            for k in parts:
                along(me, me, h, k, step).start()
        for k in range(3):
            across_start(me, me, k)
        local().start()
        for d in range(ROUNDS):
            count_copy(d).start()
        pending = [me]
        for turn, group in enumerate(ARRIVE[me]):
            for k in range(3):
                for s, h, step in group:
                    zr_wait(s, h, k)
                    if step:
                        along(me, s, h, k, step).start()
                    if h == me // 2:
                        across_start(me, s, k)
            if turn == 0:
                for h, step, parts in LATE[me]:
                    for k in parts:
                        along(me, me, h, k, step).start()
            pass_on(pending.pop(0))
            pending.extend(s for s, h, step in group if h == me // 2)
        for due in pending:
            pass_on(due)
        for s, h in LAST[me]:
            for k in range(3):
                zr_wait(s, h, k)

    def zr_wait(s, h, k):
        remote(own.at[s, h, k], own.at[s, h, k], zs.at[0, s, h, k], zr.at[s, h, k],
               (b, lax.rem(z + 1, reps))).wait_recv()

    def pr_wait(d, s, k):
        remote(part.at[d, s, k], part.at[d, s, k], xs.at[0, s, k], pr.at[d, s, k],
               (b, lax.rem(z + 1, reps))).wait_recv()

    def finish(me):
        for h, step, parts in FIRST[me] + LATE[me]:
            for k in parts:
                along(me, me, h, k, step).wait_send()
        for group in ARRIVE[me]:
            for s, h, step in group:
                if step:
                    for k in range(3):
                        along(me, s, h, k, step).wait_send()
        for s in range(reps):
            for k in range(3):
                first, second = across(me, s, k)
                first.wait_send()
                relay(s, k).wait_send()

                @pl.when(jnp.logical_not(bent))
                def _(second=second):
                    second.wait_send()

                @pl.when(bends)
                def _(s=s, k=k):
                    bend(s, k).wait_send()

    for me in range(reps):
        @pl.when(z == me)
        def _(me=me):
            program(me)

    local().wait()
    full[...] = jnp.zeros_like(full)
    gh[...] = jnp.zeros_like(gh)
    gl[...] = jnp.zeros_like(gl)
    fsq[...] = jnp.zeros_like(fsq)
    for k in range(3):
        mean = sum(jnp.sum(own[s, fh, k], axis=0, keepdims=True) for s in range(reps)) / natom
        for s in range(reps):
            full[s * pitch:s * pitch + atoms, :] = own[s, fh, k] - mean
        turned = full[...].T
        fsq[...] += jnp.broadcast_to(jnp.sum(turned * turned, axis=1, keepdims=True), fsq.shape)
        high, low = split(turned)
        fth[k * half:(k + 1) * half, :] = high
        ftl[k * half:(k + 1) * half, :] = low
    fsq[...] = fsq[...] / natom
    for d in range(ROUNDS):
        count_copy(d).wait_recv()

    def block(turn, carry):
        d = lax.rem(turn + 1, ROUNDS)

        @pl.when((d == 0) | ((d == 2) & jnp.logical_not(bends)))
        def _():
            for s in range(reps):
                for k in range(3):
                    pr_wait(d, s, k)

        square = jnp.zeros((1, half), jnp.float32)
        for k in range(3):
            mean = sum(jnp.sum(part[d, s, k], axis=0, keepdims=True) for s in range(reps)) / natom
            for s in range(reps):
                centered = part[d, s, k] - mean
                square = square + jnp.sum(centered * centered, axis=0, keepdims=True)
                high, low = split(centered)
                gh[s * pitch:s * pitch + atoms, k * half:(k + 1) * half] = high
                gl[s * pitch:s * pitch + atoms, k * half:(k + 1) * half] = low
        square = square / natom
        product = functools.partial(jnp.dot, preferred_element_type=jnp.float32)
        cov[...] = (product(fth[...], gh[...]) + product(fth[...], gl[...])
                    + product(ftl[...], gh[...])) / natom
        rows = 16

        def chunk(i, inner):
            r = pl.multiple_of(i * rows, rows)
            m = [[cov[pl.ds(k * half + r, rows), l * half:(l + 1) * half] for l in range(3)]
                 for k in range(3)]
            total = fsq[pl.ds(r, rows), :] + square
            frame = fh * half + r + lax.broadcasted_iota(jnp.int32, (rows, half), 0)
            other = gside * half + lax.broadcasted_iota(jnp.int32, (rows, half), 1)
            mask = (frame < cnt[0:1, :]) & (other < pcnt[d, 0:1, :])
            dev[d, pl.ds(r, rows), :] = jnp.where(mask, deviation(m, total), 0.0)
            return inner

        lax.fori_loop(0, half // rows, chunk, 0)
        devt[d] = dev[d].T
        for j in range(2):
            ahead_copy(d, j).start()

            @pl.when(z != 2 * fh + j)
            def _(j=j):
                behind_copy(d, j).start()

            @pl.when(z == 2 * fh + j)
            def _(j=j):
                behind[d, :, cols] = dev[d, j * quarter:(j + 1) * quarter, :]
        return carry

    lax.fori_loop(0, ROUNDS, block, 0)
    for me in range(reps):
        @pl.when(z == me)
        def _(me=me):
            finish(me)
    for d in range(ROUNDS):
        count_copy(d).wait_send()
        for j in range(2):
            ahead_copy(d, j).wait_send()

            @pl.when(z != 2 * fh + j)
            def _(d=d, j=j):
                behind_copy(d, j).wait_send()

            @pl.when(z != z // 2 + 2 * j)
            def _(d=d, j=j):
                remote(dev.at[d, pl.ds(0, quarter)], behind.at[d, :, pl.ds(j * half, half)],
                       os.at[d, 2], br.at[d, j], (at(1), z)).wait_recv()

            remote(devt.at[d, pl.ds(0, quarter)], ahead.at[d, :, pl.ds(j * half, half)],
                   os.at[d, 0], ar.at[d, j], (at(1), z)).wait_recv()


def shards(n, reps, coords, frame_count):
    atoms, frames = coords.shape[1], coords.shape[2]
    half = frames // 2
    depth = ((atoms + 15) // 16 * 16 * reps + 127) // 128 * 128
    counts = jnp.broadcast_to(frame_count.astype(jnp.int32)[:, None], (8, half))
    f32, bf16 = jnp.float32, jnp.bfloat16
    dma = pltpu.SemaphoreType.DMA
    vmem = pl.BlockSpec(memory_space=pltpu.VMEM)
    result = jax.ShapeDtypeStruct((ROUNDS, frames // reps, frames), f32)
    return pl.pallas_call(
        functools.partial(kernel, n, reps),
        out_shape=(result, result),
        in_specs=[pl.BlockSpec(memory_space=pl.ANY), vmem],
        out_specs=(vmem, vmem),
        scratch_shapes=[
            pltpu.VMEM((reps, 2, 3, atoms, half), f32),
            pltpu.VMEM((ROUNDS, reps, 3, atoms, half), f32),
            pltpu.VMEM((ROUNDS, 8, half), jnp.int32),
            pltpu.VMEM((depth, half), f32),
            pltpu.VMEM((3 * half, depth), bf16),
            pltpu.VMEM((3 * half, depth), bf16),
            pltpu.VMEM((depth, 3 * half), bf16),
            pltpu.VMEM((depth, 3 * half), bf16),
            pltpu.VMEM((3 * half, 3 * half), f32),
            pltpu.VMEM((half, half), f32),
            pltpu.VMEM((ROUNDS, half, half), f32),
            pltpu.VMEM((ROUNDS, half, half), f32),
            dma((2, reps, 2, 3)),
            dma((reps, 2, 3)),
            dma((4, reps, 3)),
            dma((ROUNDS, reps, 3)),
            dma((ROUNDS,)),
            dma((ROUNDS,)),
            dma((ROUNDS, 4)),
            dma((ROUNDS, 2)),
            dma((ROUNDS, 2)),
            dma(()),
        ],
        compiler_params=pltpu.CompilerParams(collective_id=0, has_side_effects=True),
    )(coords, counts)


def solution(mesh):
    in_specs = (P(None, "rep", "blk"), P("blk"))
    out_specs = (P(None, ("blk", "rep"), None), P(None, ("blk", "rep"), None))
    body = functools.partial(shards, mesh.shape["blk"], mesh.shape["rep"])
    return jax.shard_map(body, mesh=mesh, in_specs=in_specs, out_specs=out_specs, check_vma=False)
```

```python
import functools

import jax
import jax.numpy as jnp
from jax import lax
from jax.experimental import pallas as pl
from jax.experimental.pallas import tpu as pltpu
from jax.sharding import PartitionSpec as P

ROUNDS = 3
NEWTON = 4
MESH = pl.DeviceIdType.MESH

ALL = (0, 1, 2)
FIRST = (
    ((1, 1, ALL), (0, 1, ALL)),
    ((1, 1, ALL), (0, -1, ALL), (0, 1, (0,))),
    ((0, -1, ALL), (1, 1, ALL), (1, -1, (0,))),
    ((0, -1, ALL), (1, -1, ALL)),
)
LATE = ((), ((0, 1, (1, 2)),), ((1, -1, (1, 2)),), ())
ARRIVE = (
    (((1, 0, 0),), ((2, 0, 0),), ((3, 0, 0),)),
    (((2, 0, -1), (0, 1, 1)), ((3, 0, -1), (0, 0, 1))),
    (((1, 1, 1), (3, 0, -1)), ((0, 1, 1), (3, 1, -1))),
    (((2, 1, 0),), ((1, 1, 0),), ((0, 1, 0),)),
)
LAST = ((), ((2, 1), (3, 1)), ((1, 0), (0, 0)), ())


def pair_minor(upper, lower, left, right):
    return upper[left] * lower[right] - upper[right] * lower[left]


def deviation(m, total):
    keyed = [
        [m[0][0] + m[1][1] + m[2][2], m[1][2] - m[2][1], m[2][0] - m[0][2], m[0][1] - m[1][0]],
        [m[1][2] - m[2][1], m[0][0] - m[1][1] - m[2][2], m[0][1] + m[1][0], m[2][0] + m[0][2]],
        [m[2][0] - m[0][2], m[0][1] + m[1][0], -m[0][0] + m[1][1] - m[2][2], m[1][2] + m[2][1]],
        [m[0][1] - m[1][0], m[2][0] + m[0][2], m[1][2] + m[2][1], -m[0][0] - m[1][1] + m[2][2]],
    ]
    top_one, top_two, low_one, low_two = keyed
    det_key = (
        pair_minor(top_one, top_two, 0, 1) * pair_minor(low_one, low_two, 2, 3)
        - pair_minor(top_one, top_two, 0, 2) * pair_minor(low_one, low_two, 1, 3)
        + pair_minor(top_one, top_two, 0, 3) * pair_minor(low_one, low_two, 1, 2)
        + pair_minor(top_one, top_two, 1, 2) * pair_minor(low_one, low_two, 0, 3)
        - pair_minor(top_one, top_two, 1, 3) * pair_minor(low_one, low_two, 0, 2)
        + pair_minor(top_one, top_two, 2, 3) * pair_minor(low_one, low_two, 0, 1)
    )
    det_three = (
        m[0][0] * (m[1][1] * m[2][2] - m[1][2] * m[2][1])
        - m[0][1] * (m[1][0] * m[2][2] - m[1][2] * m[2][0])
        + m[0][2] * (m[1][0] * m[2][1] - m[1][1] * m[2][0])
    )
    square_sum = m[0][0] * m[0][0]
    for first in range(3):
        for second in range(3):
            if first + second > 0:
                square_sum = square_sum + m[first][second] * m[first][second]
    second_coef = -2.0 * square_sum
    first_coef = -8.0 * det_three
    largest = 0.5 * total
    for newton_step in range(NEWTON):
        squared = largest * largest
        polynomial = squared * squared + second_coef * squared + first_coef * largest + det_key
        derivative = 4.0 * squared * largest + 2.0 * second_coef * largest + first_coef
        largest = largest - polynomial / derivative
    return total - 2.0 * largest


def split(value):
    high = value.astype(jnp.bfloat16)
    low = (value - high.astype(jnp.float32)).astype(jnp.bfloat16)
    return high, low


def kernel(n, reps, coords, cnt, behind, ahead, own, part, pcnt, full, fth, ftl, gh, gl, cov,
           fsq, dev, devt, zs, zr, xs, pr, cs, cr, os, br, ar, ls):
    b = lax.axis_index("blk")
    z = lax.axis_index("rep")
    par = lax.rem(b, 2)
    bent = lax.rem(b // 2, 2) * par == 1
    bends = lax.rem(b // 2, 2) * (1 - par) == 1
    atoms = coords.shape[1]
    half = coords.shape[2] // 2
    quarter = half // 2
    pitch = (atoms + 15) // 16 * 16
    natom = atoms * reps
    fh = lax.rem(z, 2)
    gside = z // 2

    def at(step):
        return lax.rem(b + step + n, n)

    barrier = pltpu.get_barrier_semaphore()
    for step in range(-ROUNDS, ROUNDS + 1):
        if step:
            pl.semaphore_signal(barrier, inc=1, device_id=(at(step), z), device_id_type=MESH)

    @pl.when(z > 0)
    def _():
        pl.semaphore_signal(barrier, inc=1, device_id=(b, z - 1), device_id_type=MESH)

    @pl.when(z < reps - 1)
    def _():
        pl.semaphore_signal(barrier, inc=1, device_id=(b, z + 1), device_id_type=MESH)

    inner = jnp.minimum(z, 1) * jnp.minimum(reps - 1 - z, 1)
    pl.semaphore_wait(barrier, 2 * ROUNDS + 1 + inner)

    def remote(src, dst, send, recv, where):
        return pltpu.make_async_remote_copy(src_ref=src, dst_ref=dst, send_sem=send, recv_sem=recv,
                                            device_id=where, device_id_type=MESH)

    def along(me, s, h, k, step):
        src = coords.at[k, :, pl.ds(h * half, half)] if s == me else own.at[s, h, k]
        return remote(src, own.at[s, h, k], zs.at[(step + 1) // 2, s, h, k], zr.at[s, h, k],
                      (b, z + step))

    def across(me, s, k):
        h = me // 2
        src = coords.at[k, :, pl.ds(h * half, half)] if s == me else own.at[s, h, k]
        slot = 2 * par
        return (
            remote(src, part.at[slot, s, k], xs.at[1, s, k], pr.at[slot, s, k], (at(1 + slot), z)),
            remote(src, part.at[1, s, k], xs.at[0, s, k], pr.at[1, s, k], (at(2), z)),
        )

    def across_start(me, s, k):
        first, second = across(me, s, k)
        first.start()

        @pl.when(jnp.logical_not(bent))
        def _():
            second.start()

    def bend(s, k):
        return remote(part.at[2, s, k], part.at[1, s, k], xs.at[3, s, k], pr.at[1, s, k],
                      (at(-1), z))

    def relay(s, k):
        slot = 2 - 2 * par
        return remote(part.at[1, s, k], part.at[slot, s, k], xs.at[2, s, k], pr.at[slot, s, k],
                      (at(1 - 2 * par), z))

    def pass_on(*sources):
        for k in range(3):
            @pl.when(bends)
            def _(k=k):
                for s in sources:
                    pr_wait(2, s, k)
                    bend(s, k).start()

            for s in sources:
                pr_wait(1, s, k)
                relay(s, k).start()

    def count_copy(d):
        return remote(cnt, pcnt.at[d], cs.at[d], cr.at[d], (at(d + 1), z))

    def local():
        return pltpu.make_async_copy(coords.at[:, :, pl.ds(pl.multiple_of(fh * half, half), half)],
                                     own.at[z, fh], ls)

    cols = pl.ds(pl.multiple_of(gside * half, half), half)

    def behind_copy(d, j):
        return remote(dev.at[d, pl.ds(j * quarter, quarter)], behind.at[d, :, cols],
                      os.at[d, 2 + j], br.at[d, gside], (b, 2 * fh + j))

    def ahead_copy(d, j):
        mine = pl.ds(pl.multiple_of(fh * half, half), half)
        return remote(devt.at[d, pl.ds(j * quarter, quarter)], ahead.at[d, :, mine],
                      os.at[d, j], ar.at[d, fh], (lax.rem(b - 1 - d + n, n), 2 * gside + j))

    def program(me):
        for h, step, parts in FIRST[me]:
            for k in parts:
                along(me, me, h, k, step).start()
        for k in range(3):
            across_start(me, me, k)
        local().start()
        for d in range(ROUNDS):
            count_copy(d).start()
        pending = [me]
        for turn, group in enumerate(ARRIVE[me]):
            for k in range(3):
                for s, h, step in group:
                    zr_wait(s, h, k)
                    if step:
                        along(me, s, h, k, step).start()
                    if h == me // 2:
                        across_start(me, s, k)
            if turn == 0:
                for h, step, parts in LATE[me]:
                    for k in parts:
                        along(me, me, h, k, step).start()
            pass_on(pending.pop(0))
            pending.extend(s for s, h, step in group if h == me // 2)
        pass_on(*pending)
        for s, h in LAST[me]:
            for k in range(3):
                zr_wait(s, h, k)

    def zr_wait(s, h, k):
        remote(own.at[s, h, k], own.at[s, h, k], zs.at[0, s, h, k], zr.at[s, h, k],
               (b, lax.rem(z + 1, reps))).wait_recv()

    def pr_wait(d, s, k):
        remote(part.at[d, s, k], part.at[d, s, k], xs.at[0, s, k], pr.at[d, s, k],
               (b, lax.rem(z + 1, reps))).wait_recv()

    def finish(me):
        for h, step, parts in FIRST[me] + LATE[me]:
            for k in parts:
                along(me, me, h, k, step).wait_send()
        for group in ARRIVE[me]:
            for s, h, step in group:
                if step:
                    for k in range(3):
                        along(me, s, h, k, step).wait_send()
        for s in range(reps):
            for k in range(3):
                first, second = across(me, s, k)
                first.wait_send()
                relay(s, k).wait_send()

                @pl.when(jnp.logical_not(bent))
                def _(second=second):
                    second.wait_send()

                @pl.when(bends)
                def _(s=s, k=k):
                    bend(s, k).wait_send()

    for me in range(reps):
        @pl.when(z == me)
        def _(me=me):
            program(me)

    local().wait()
    full[...] = jnp.zeros_like(full)
    gh[...] = jnp.zeros_like(gh)
    gl[...] = jnp.zeros_like(gl)
    fsq[...] = jnp.zeros_like(fsq)
    for k in range(3):
        mean = sum(jnp.sum(own[s, fh, k], axis=0, keepdims=True) for s in range(reps)) / natom
        for s in range(reps):
            full[s * pitch:s * pitch + atoms, :] = own[s, fh, k] - mean
        turned = full[...].T
        fsq[...] += jnp.broadcast_to(jnp.sum(turned * turned, axis=1, keepdims=True), fsq.shape)
        high, low = split(turned)
        fth[k * half:(k + 1) * half, :] = high
        ftl[k * half:(k + 1) * half, :] = low
    fsq[...] = fsq[...] / natom
    for d in range(ROUNDS):
        count_copy(d).wait_recv()

    def block(turn, carry):
        d = lax.rem(turn + 1, ROUNDS)

        @pl.when((d == 0) | ((d == 2) & jnp.logical_not(bends)))
        def _():
            for s in range(reps):
                for k in range(3):
                    pr_wait(d, s, k)

        square = jnp.zeros((1, half), jnp.float32)
        for k in range(3):
            mean = sum(jnp.sum(part[d, s, k], axis=0, keepdims=True) for s in range(reps)) / natom
            for s in range(reps):
                centered = part[d, s, k] - mean
                square = square + jnp.sum(centered * centered, axis=0, keepdims=True)
                high, low = split(centered)
                gh[s * pitch:s * pitch + atoms, k * half:(k + 1) * half] = high
                gl[s * pitch:s * pitch + atoms, k * half:(k + 1) * half] = low
        square = square / natom
        product = functools.partial(jnp.dot, preferred_element_type=jnp.float32)
        cov[...] = (product(fth[...], gh[...]) + product(fth[...], gl[...])
                    + product(ftl[...], gh[...])) / natom
        rows = 16

        def chunk(i, inner):
            r = pl.multiple_of(i * rows, rows)
            m = [[cov[pl.ds(k * half + r, rows), l * half:(l + 1) * half] for l in range(3)]
                 for k in range(3)]
            total = fsq[pl.ds(r, rows), :] + square
            frame = fh * half + r + lax.broadcasted_iota(jnp.int32, (rows, half), 0)
            other = gside * half + lax.broadcasted_iota(jnp.int32, (rows, half), 1)
            mask = (frame < cnt[0:1, :]) & (other < pcnt[d, 0:1, :])
            dev[d, pl.ds(r, rows), :] = jnp.where(mask, deviation(m, total), 0.0)
            return inner

        lax.fori_loop(0, half // rows, chunk, 0)
        devt[d] = dev[d].T
        for j in range(2):
            ahead_copy(d, j).start()

            @pl.when(z != 2 * fh + j)
            def _(j=j):
                behind_copy(d, j).start()

            @pl.when(z == 2 * fh + j)
            def _(j=j):
                behind[d, :, cols] = dev[d, j * quarter:(j + 1) * quarter, :]
        return carry

    lax.fori_loop(0, ROUNDS, block, 0)
    for me in range(reps):
        @pl.when(z == me)
        def _(me=me):
            finish(me)
    for d in range(ROUNDS):
        count_copy(d).wait_send()
        for j in range(2):
            ahead_copy(d, j).wait_send()

            @pl.when(z != 2 * fh + j)
            def _(d=d, j=j):
                behind_copy(d, j).wait_send()

            @pl.when(z != z // 2 + 2 * j)
            def _(d=d, j=j):
                remote(dev.at[d, pl.ds(0, quarter)], behind.at[d, :, pl.ds(j * half, half)],
                       os.at[d, 2], br.at[d, j], (at(1), z)).wait_recv()

            remote(devt.at[d, pl.ds(0, quarter)], ahead.at[d, :, pl.ds(j * half, half)],
                   os.at[d, 0], ar.at[d, j], (at(1), z)).wait_recv()


def shards(n, reps, coords, frame_count):
    atoms, frames = coords.shape[1], coords.shape[2]
    half = frames // 2
    depth = ((atoms + 15) // 16 * 16 * reps + 127) // 128 * 128
    counts = jnp.broadcast_to(frame_count.astype(jnp.int32)[:, None], (8, half))
    f32, bf16 = jnp.float32, jnp.bfloat16
    dma = pltpu.SemaphoreType.DMA
    vmem = pl.BlockSpec(memory_space=pltpu.VMEM)
    result = jax.ShapeDtypeStruct((ROUNDS, frames // reps, frames), f32)
    return pl.pallas_call(
        functools.partial(kernel, n, reps),
        out_shape=(result, result),
        in_specs=[pl.BlockSpec(memory_space=pl.ANY), vmem],
        out_specs=(vmem, vmem),
        scratch_shapes=[
            pltpu.VMEM((reps, 2, 3, atoms, half), f32),
            pltpu.VMEM((ROUNDS, reps, 3, atoms, half), f32),
            pltpu.VMEM((ROUNDS, 8, half), jnp.int32),
            pltpu.VMEM((depth, half), f32),
            pltpu.VMEM((3 * half, depth), bf16),
            pltpu.VMEM((3 * half, depth), bf16),
            pltpu.VMEM((depth, 3 * half), bf16),
            pltpu.VMEM((depth, 3 * half), bf16),
            pltpu.VMEM((3 * half, 3 * half), f32),
            pltpu.VMEM((half, half), f32),
            pltpu.VMEM((ROUNDS, half, half), f32),
            pltpu.VMEM((ROUNDS, half, half), f32),
            dma((2, reps, 2, 3)),
            dma((reps, 2, 3)),
            dma((4, reps, 3)),
            dma((ROUNDS, reps, 3)),
            dma((ROUNDS,)),
            dma((ROUNDS,)),
            dma((ROUNDS, 4)),
            dma((ROUNDS, 2)),
            dma((ROUNDS, 2)),
            dma(()),
        ],
        compiler_params=pltpu.CompilerParams(collective_id=0, has_side_effects=True),
    )(coords, counts)


def solution(mesh):
    in_specs = (P(None, "rep", "blk"), P("blk"))
    out_specs = (P(None, ("blk", "rep"), None), P(None, ("blk", "rep"), None))
    body = functools.partial(shards, mesh.shape["blk"], mesh.shape["rep"])
    return jax.shard_map(body, mesh=mesh, in_specs=in_specs, out_specs=out_specs, check_vma=False)
```

```python
import functools

import jax
import jax.numpy as jnp
from jax import lax
from jax.experimental import pallas as pl
from jax.experimental.pallas import tpu as pltpu
from jax.sharding import PartitionSpec as P

ROUNDS = 3
NEWTON = 4
MESH = pl.DeviceIdType.MESH

ALL = (0, 1, 2)
FIRST = (
    ((1, 1, ALL), (0, 1, ALL)),
    ((1, 1, ALL), (0, -1, ALL), (0, 1, (0,))),
    ((0, -1, ALL), (1, 1, ALL), (1, -1, (0,))),
    ((0, -1, ALL), (1, -1, ALL)),
)
LATE = ((), ((0, 1, (1, 2)),), ((1, -1, (1, 2)),), ())
ARRIVE = (
    (((1, 0, 0),), ((2, 0, 0),), ((3, 0, 0),)),
    (((2, 0, -1), (0, 1, 1)), ((3, 0, -1), (0, 0, 1))),
    (((1, 1, 1), (3, 0, -1)), ((0, 1, 1), (3, 1, -1))),
    (((2, 1, 0),), ((1, 1, 0),), ((0, 1, 0),)),
)
LAST = ((), ((2, 1), (3, 1)), ((1, 0), (0, 0)), ())


def pair_minor(upper, lower, left, right):
    return upper[left] * lower[right] - upper[right] * lower[left]


def deviation(m, total):
    keyed = [
        [m[0][0] + m[1][1] + m[2][2], m[1][2] - m[2][1], m[2][0] - m[0][2], m[0][1] - m[1][0]],
        [m[1][2] - m[2][1], m[0][0] - m[1][1] - m[2][2], m[0][1] + m[1][0], m[2][0] + m[0][2]],
        [m[2][0] - m[0][2], m[0][1] + m[1][0], -m[0][0] + m[1][1] - m[2][2], m[1][2] + m[2][1]],
        [m[0][1] - m[1][0], m[2][0] + m[0][2], m[1][2] + m[2][1], -m[0][0] - m[1][1] + m[2][2]],
    ]
    top_one, top_two, low_one, low_two = keyed
    det_key = (
        pair_minor(top_one, top_two, 0, 1) * pair_minor(low_one, low_two, 2, 3)
        - pair_minor(top_one, top_two, 0, 2) * pair_minor(low_one, low_two, 1, 3)
        + pair_minor(top_one, top_two, 0, 3) * pair_minor(low_one, low_two, 1, 2)
        + pair_minor(top_one, top_two, 1, 2) * pair_minor(low_one, low_two, 0, 3)
        - pair_minor(top_one, top_two, 1, 3) * pair_minor(low_one, low_two, 0, 2)
        + pair_minor(top_one, top_two, 2, 3) * pair_minor(low_one, low_two, 0, 1)
    )
    det_three = (
        m[0][0] * (m[1][1] * m[2][2] - m[1][2] * m[2][1])
        - m[0][1] * (m[1][0] * m[2][2] - m[1][2] * m[2][0])
        + m[0][2] * (m[1][0] * m[2][1] - m[1][1] * m[2][0])
    )
    square_sum = m[0][0] * m[0][0]
    for first in range(3):
        for second in range(3):
            if first + second > 0:
                square_sum = square_sum + m[first][second] * m[first][second]
    second_coef = -2.0 * square_sum
    first_coef = -8.0 * det_three
    largest = 0.5 * total
    for newton_step in range(NEWTON):
        squared = largest * largest
        polynomial = squared * squared + second_coef * squared + first_coef * largest + det_key
        derivative = 4.0 * squared * largest + 2.0 * second_coef * largest + first_coef
        largest = largest - polynomial / derivative
    return total - 2.0 * largest


def split(value):
    high = value.astype(jnp.bfloat16)
    low = (value - high.astype(jnp.float32)).astype(jnp.bfloat16)
    return high, low


def kernel(n, reps, coords, cnt, behind, ahead, own, part, pcnt, full, fth, ftl, gh, gl, cov,
           fsq, dev, devt, zs, zr, xs, pr, cs, cr, os, br, ar, ls):
    b = lax.axis_index("blk")
    z = lax.axis_index("rep")
    par = lax.rem(b, 2)
    bent = lax.rem(b // 2, 2) * par == 1
    bends = lax.rem(b // 2, 2) * (1 - par) == 1
    atoms = coords.shape[1]
    half = coords.shape[2] // 2
    quarter = half // 2
    pitch = (atoms + 15) // 16 * 16
    natom = atoms * reps
    fh = lax.rem(z, 2)
    gside = z // 2

    def at(step):
        return lax.rem(b + step + n, n)

    barrier = pltpu.get_barrier_semaphore()
    for step in range(-ROUNDS, ROUNDS + 1):
        if step:
            pl.semaphore_signal(barrier, inc=1, device_id=(at(step), z), device_id_type=MESH)

    @pl.when(z > 0)
    def _():
        pl.semaphore_signal(barrier, inc=1, device_id=(b, z - 1), device_id_type=MESH)

    @pl.when(z < reps - 1)
    def _():
        pl.semaphore_signal(barrier, inc=1, device_id=(b, z + 1), device_id_type=MESH)

    inner = jnp.minimum(z, 1) * jnp.minimum(reps - 1 - z, 1)
    pl.semaphore_wait(barrier, 2 * ROUNDS + 1 + inner)

    def remote(src, dst, send, recv, where):
        return pltpu.make_async_remote_copy(src_ref=src, dst_ref=dst, send_sem=send, recv_sem=recv,
                                            device_id=where, device_id_type=MESH)

    def along(me, s, h, k, step):
        src = coords.at[k, :, pl.ds(h * half, half)] if s == me else own.at[s, h, k]
        return remote(src, own.at[s, h, k], zs.at[(step + 1) // 2, s, h, k], zr.at[s, h, k],
                      (b, z + step))

    def across(me, s, k):
        h = me // 2
        src = coords.at[k, :, pl.ds(h * half, half)] if s == me else own.at[s, h, k]
        slot = 2 * par
        return (
            remote(src, part.at[slot, s, k], xs.at[1, s, k], pr.at[slot, s, k], (at(1 + slot), z)),
            remote(src, part.at[1, s, k], xs.at[0, s, k], pr.at[1, s, k], (at(2), z)),
        )

    def across_start(me, s, k):
        first, second = across(me, s, k)
        first.start()

        @pl.when(jnp.logical_not(bent))
        def _():
            second.start()

    def bend(s, k):
        return remote(part.at[2, s, k], part.at[1, s, k], xs.at[3, s, k], pr.at[1, s, k],
                      (at(-1), z))

    def relay(s, k):
        slot = 2 - 2 * par
        return remote(part.at[1, s, k], part.at[slot, s, k], xs.at[2, s, k], pr.at[slot, s, k],
                      (at(1 - 2 * par), z))

    def pass_on(*sources):
        for k in range(3):
            @pl.when(bends)
            def _(k=k):
                for s in sources:
                    pr_wait(2, s, k)
                    bend(s, k).start()

            for s in sources:
                pr_wait(1, s, k)
                relay(s, k).start()

    def count_copy(d):
        return remote(cnt, pcnt.at[d], cs.at[d], cr.at[d], (at(d + 1), z))

    def local():
        return pltpu.make_async_copy(coords.at[:, :, pl.ds(pl.multiple_of(fh * half, half), half)],
                                     own.at[z, fh], ls)

    cols = pl.ds(pl.multiple_of(gside * half, half), half)

    def behind_copy(d, j):
        return remote(dev.at[d, pl.ds(j * quarter, quarter)], behind.at[d, :, cols],
                      os.at[d, 2 + j], br.at[d, gside], (b, 2 * fh + j))

    def ahead_copy(d, j):
        mine = pl.ds(pl.multiple_of(fh * half, half), half)
        return remote(devt.at[d, pl.ds(j * quarter, quarter)], ahead.at[d, :, mine],
                      os.at[d, j], ar.at[d, fh], (lax.rem(b - 1 - d + n, n), 2 * gside + j))

    def program(me):
        for h, step, parts in FIRST[me]:
            for k in parts:
                along(me, me, h, k, step).start()
        for k in range(3):
            across_start(me, me, k)
        local().start()
        for d in range(ROUNDS):
            count_copy(d).start()
        pending = [me]
        for turn, group in enumerate(ARRIVE[me]):
            for k in range(3):
                for s, h, step in group:
                    zr_wait(s, h, k)
                    if step:
                        along(me, s, h, k, step).start()
                    if h == me // 2:
                        across_start(me, s, k)
            if turn == 0:
                for h, step, parts in LATE[me]:
                    for k in parts:
                        along(me, me, h, k, step).start()
            pass_on(pending.pop(0))
            pending.extend(s for s, h, step in group if h == me // 2)
        pass_on(*pending)
        for s, h in LAST[me]:
            for k in range(3):
                zr_wait(s, h, k)

    def zr_wait(s, h, k):
        remote(own.at[s, h, k], own.at[s, h, k], zs.at[0, s, h, k], zr.at[s, h, k],
               (b, lax.rem(z + 1, reps))).wait_recv()

    def pr_wait(d, s, k):
        remote(part.at[d, s, k], part.at[d, s, k], xs.at[0, s, k], pr.at[d, s, k],
               (b, lax.rem(z + 1, reps))).wait_recv()

    def finish(me):
        for h, step, parts in FIRST[me] + LATE[me]:
            for k in parts:
                along(me, me, h, k, step).wait_send()
        for group in ARRIVE[me]:
            for s, h, step in group:
                if step:
                    for k in range(3):
                        along(me, s, h, k, step).wait_send()
        for s in range(reps):
            for k in range(3):
                first, second = across(me, s, k)
                first.wait_send()
                relay(s, k).wait_send()

                @pl.when(jnp.logical_not(bent))
                def _(second=second):
                    second.wait_send()

                @pl.when(bends)
                def _(s=s, k=k):
                    bend(s, k).wait_send()

    for me in range(reps):
        @pl.when(z == me)
        def _(me=me):
            program(me)

    local().wait()
    full[...] = jnp.zeros_like(full)
    gh[...] = jnp.zeros_like(gh)
    gl[...] = jnp.zeros_like(gl)
    fsq[...] = jnp.zeros_like(fsq)
    for k in range(3):
        mean = sum(jnp.sum(own[s, fh, k], axis=0, keepdims=True) for s in range(reps)) / natom
        for s in range(reps):
            full[s * pitch:s * pitch + atoms, :] = own[s, fh, k] - mean
        turned = full[...].T
        fsq[...] += jnp.broadcast_to(jnp.sum(turned * turned, axis=1, keepdims=True), fsq.shape)
        high, low = split(turned)
        fth[k * half:(k + 1) * half, :] = high
        ftl[k * half:(k + 1) * half, :] = low
    fsq[...] = fsq[...] / natom
    for d in range(ROUNDS):
        count_copy(d).wait_recv()

    def block(turn, carry):
        d = lax.rem(turn + 1, ROUNDS)

        @pl.when((d == 0) | ((d == 2) & jnp.logical_not(bends)))
        def _():
            for s in range(reps):
                for k in range(3):
                    pr_wait(d, s, k)

        square = jnp.zeros((1, half), jnp.float32)
        for k in range(3):
            mean = sum(jnp.sum(part[d, s, k], axis=0, keepdims=True) for s in range(reps)) / natom
            for s in range(reps):
                centered = part[d, s, k] - mean
                square = square + jnp.sum(centered * centered, axis=0, keepdims=True)
                high, low = split(centered)
                gh[s * pitch:s * pitch + atoms, k * half:(k + 1) * half] = high
                gl[s * pitch:s * pitch + atoms, k * half:(k + 1) * half] = low
        square = square / natom
        product = functools.partial(jnp.dot, preferred_element_type=jnp.float32)
        cov[...] = (product(fth[...], gh[...]) + product(fth[...], gl[...])
                    + product(ftl[...], gh[...])) / natom
        rows = half // 4

        def chunk(i, inner):
            r = pl.multiple_of(i * rows, rows)
            m = [[cov[pl.ds(k * half + r, rows), l * half:(l + 1) * half] for l in range(3)]
                 for k in range(3)]
            total = fsq[pl.ds(r, rows), :] + square
            frame = fh * half + r + lax.broadcasted_iota(jnp.int32, (rows, half), 0)
            other = gside * half + lax.broadcasted_iota(jnp.int32, (rows, half), 1)
            mask = (frame < cnt[0:1, :]) & (other < pcnt[d, 0:1, :])
            dev[d, pl.ds(r, rows), :] = jnp.where(mask, deviation(m, total), 0.0)
            return inner

        lax.fori_loop(0, half // rows, chunk, 0)
        devt[d] = dev[d].T
        for j in range(2):
            ahead_copy(d, j).start()

            @pl.when(z != 2 * fh + j)
            def _(j=j):
                behind_copy(d, j).start()

            @pl.when(z == 2 * fh + j)
            def _(j=j):
                behind[d, :, cols] = dev[d, j * quarter:(j + 1) * quarter, :]
        return carry

    lax.fori_loop(0, ROUNDS, block, 0)
    for me in range(reps):
        @pl.when(z == me)
        def _(me=me):
            finish(me)
    for d in range(ROUNDS):
        count_copy(d).wait_send()
        for j in range(2):
            ahead_copy(d, j).wait_send()

            @pl.when(z != 2 * fh + j)
            def _(d=d, j=j):
                behind_copy(d, j).wait_send()

            @pl.when(z != z // 2 + 2 * j)
            def _(d=d, j=j):
                remote(dev.at[d, pl.ds(0, quarter)], behind.at[d, :, pl.ds(j * half, half)],
                       os.at[d, 2], br.at[d, j], (at(1), z)).wait_recv()

            remote(devt.at[d, pl.ds(0, quarter)], ahead.at[d, :, pl.ds(j * half, half)],
                   os.at[d, 0], ar.at[d, j], (at(1), z)).wait_recv()


def shards(n, reps, coords, frame_count):
    atoms, frames = coords.shape[1], coords.shape[2]
    half = frames // 2
    depth = ((atoms + 15) // 16 * 16 * reps + 127) // 128 * 128
    counts = jnp.broadcast_to(frame_count.astype(jnp.int32)[:, None], (8, half))
    f32, bf16 = jnp.float32, jnp.bfloat16
    dma = pltpu.SemaphoreType.DMA
    vmem = pl.BlockSpec(memory_space=pltpu.VMEM)
    result = jax.ShapeDtypeStruct((ROUNDS, frames // reps, frames), f32)
    return pl.pallas_call(
        functools.partial(kernel, n, reps),
        out_shape=(result, result),
        in_specs=[pl.BlockSpec(memory_space=pl.ANY), vmem],
        out_specs=(vmem, vmem),
        scratch_shapes=[
            pltpu.VMEM((reps, 2, 3, atoms, half), f32),
            pltpu.VMEM((ROUNDS, reps, 3, atoms, half), f32),
            pltpu.VMEM((ROUNDS, 8, half), jnp.int32),
            pltpu.VMEM((depth, half), f32),
            pltpu.VMEM((3 * half, depth), bf16),
            pltpu.VMEM((3 * half, depth), bf16),
            pltpu.VMEM((depth, 3 * half), bf16),
            pltpu.VMEM((depth, 3 * half), bf16),
            pltpu.VMEM((3 * half, 3 * half), f32),
            pltpu.VMEM((half, half), f32),
            pltpu.VMEM((ROUNDS, half, half), f32),
            pltpu.VMEM((ROUNDS, half, half), f32),
            dma((2, reps, 2, 3)),
            dma((reps, 2, 3)),
            dma((4, reps, 3)),
            dma((ROUNDS, reps, 3)),
            dma((ROUNDS,)),
            dma((ROUNDS,)),
            dma((ROUNDS, 4)),
            dma((ROUNDS, 2)),
            dma((ROUNDS, 2)),
            dma(()),
        ],
        compiler_params=pltpu.CompilerParams(collective_id=0, has_side_effects=True),
    )(coords, counts)


def solution(mesh):
    in_specs = (P(None, "rep", "blk"), P("blk"))
    out_specs = (P(None, ("blk", "rep"), None), P(None, ("blk", "rep"), None))
    body = functools.partial(shards, mesh.shape["blk"], mesh.shape["rep"])
    return jax.shard_map(body, mesh=mesh, in_specs=in_specs, out_specs=out_specs, check_vma=False)
```
